32 devices in a mesh: shot: 8 (over y, x, core), rcv: 4 (over z).
Axes of the slice: x: 2, y: 2, z: 4, core: 2. Of those that a mesh axis runs over, the one named last changes fastest.
Arguments:
- spectra: bfloat16 [4, 2, 2048, 2048], P(None, None, 'shot', 'rcv'), may hold values from -6 to 6
Outputs:
- multiples: float32 [4, 2, 2048, 2048], P('rcv', None, 'shot')
The draws below stay inside these ranges and needn't reach their ends.
All inputs are finite; a program needn't handle non-finite values.
Results may differ from the reference program's by a relative error of at most 0.0003.
Values may be sent and summed in bfloat16 or wider, within the bound.
A program may use at most 128 MiB of HBM per device.

```python
import math
import jax
import jax.numpy as jnp
from jax import lax

NG = 2048
NFREQ = 4


def block_scale(own_key, dims, split, least, largest):
    factor_of = 1.0
    for position, blocks in split:
        draws = jax.random.uniform(jax.random.fold_in(jax.random.fold_in(own_key, 6), position), (blocks,), jnp.float32, least / len(split), largest / len(split))
        factor_of = factor_of * jnp.repeat(jnp.exp(draws), dims[position] // blocks).reshape((-1,) + (1,) * (len(dims) - 1 - position))
    return factor_of


def normal_values(rng, extent, spread, bound, split=(), kind=jnp.bfloat16):
    entries = spread * jax.random.normal(rng, extent, jnp.float32)
    if split:
        entries = entries * block_scale(rng, extent, split, -0.22, 0.18)
    return jnp.clip(entries, -bound, bound).astype(kind)


def setup_inputs(seed: int = 0) -> dict:
    key_list = jax.random.split(jax.random.key(seed), 2)
    spectra = normal_values(key_list[0], (NFREQ, 2, NG, NG), 1.0, 6.0, ((2, 8), (3, 4)))
    return dict(spectra=spectra)


def one_frequency(pair):
    real_part = pair[0].astype(jnp.float32)
    imag_part = pair[1].astype(jnp.float32)
    real_out = jnp.dot(real_part, real_part, preferred_element_type=jnp.float32) - jnp.dot(imag_part, imag_part, preferred_element_type=jnp.float32)
    imag_out = jnp.dot(real_part, imag_part, preferred_element_type=jnp.float32) + jnp.dot(imag_part, real_part, preferred_element_type=jnp.float32)
    return jnp.stack([real_out, imag_out], axis=0)

def reference(spectra):
    spectral_products = lax.map(one_frequency, spectra)
    return spectral_products * (-1.0 / math.sqrt(NG))
```

```python
import functools
import math

import jax
import jax.numpy as jnp
from jax import lax
from jax.experimental import pallas as pl
from jax.experimental.pallas import tpu as pltpu
from jax.sharding import PartitionSpec as P

MESH = pl.DeviceIdType.MESH
PLANE = 8
LINE = 4

FROM_X, FROM_Y, DIAGONAL = 0, 2, 4
CORE_OWN, CORE_X, CORE_Y, CORE_DIAGONAL = 6, 8, 10, 12
KINDS = 14


def kernel(rows, cols, scale, x_ref, out_ref, g, own_sem, line_send, line_recv, send, recv):
    s, z = lax.axis_index("shot"), lax.axis_index("rcv")
    y, x, c = s // 4, (s // 2) % 2, s % 2
    sx = y * 4 + (1 - x) * 2 + c
    sy = (1 - y) * 4 + x * 2 + c
    sd = (1 - y) * 4 + (1 - x) * 2 + c
    sc = y * 4 + x * 2 + (1 - c)
    half = z // 2
    u = z + half * (3 - 2 * z)

    def mirrored(v):
        return v + half * (3 - 2 * v)

    order = [z, mirrored(1 - u), mirrored(2), mirrored(3)]
    others = order[1:]

    barrier = pltpu.get_barrier_semaphore()
    for peer in (sx, sy, sc):
        pl.semaphore_signal(barrier, inc=1, device_id=(peer, z), device_id_type=MESH)
    for peer in others:
        pl.semaphore_signal(barrier, inc=1, device_id=(s, peer), device_id_type=MESH)
    pl.semaphore_wait(barrier, 6)

    def block(column, part, shot):
        return g.at[part, column, pl.ds(shot * rows, rows), :]

    def along_line(peer, part):
        return pltpu.make_async_remote_copy(
            src_ref=x_ref.at[peer, part],
            dst_ref=block(z, part, s),
            send_sem=line_send.at[peer, part],
            recv_sem=line_recv.at[z, part],
            device_id=(s, peer),
            device_id_type=MESH,
        )

    def line_arrival(source, part):
        return pltpu.make_async_remote_copy(
            src_ref=x_ref.at[source, part],
            dst_ref=block(source, part, s),
            send_sem=line_send.at[source, part],
            recv_sem=line_recv.at[source, part],
            device_id=(s, source),
            device_id_type=MESH,
        )

    started = []

    def push(rnd, kind, part, shot, target, source=None):
        place = block(order[rnd], part, shot)
        copy = pltpu.make_async_remote_copy(
            src_ref=place if source is None else source,
            dst_ref=place,
            send_sem=send.at[rnd, kind + part],
            recv_sem=recv.at[rnd, kind + part],
            device_id=(target, z),
            device_id_type=MESH,
        )
        copy.start()
        started.append(copy)

    def arrive(rnd, kind, part, shot):
        place = block(order[rnd], part, shot)
        pltpu.make_async_remote_copy(
            src_ref=place,
            dst_ref=place,
            send_sem=send.at[rnd, kind + part],
            recv_sem=recv.at[rnd, kind + part],
            device_id=(sx, z),
            device_id_type=MESH,
        ).wait_recv()

    def send_own(rnd):
        for part, kind, target in ((0, FROM_X, sx), (1, FROM_Y, sy), (1, FROM_X, sx), (0, FROM_Y, sy)):
            push(rnd, kind, part, s, target, x_ref.at[z, part] if rnd == 0 else None)
        for part in range(2):
            push(rnd, CORE_OWN, part, s, sc, x_ref.at[z, part] if rnd == 0 else None)

    def relay(rnd):
        arrive(rnd, FROM_X, 0, sx)
        push(rnd, DIAGONAL, 0, sx, sy)
        arrive(rnd, FROM_Y, 1, sy)
        push(rnd, DIAGONAL, 1, sy, sx)
        push(rnd, CORE_X, 0, sx, sc)
        push(rnd, CORE_Y, 1, sy, sc)

    def finish_direct(rnd):
        arrive(rnd, FROM_X, 1, sx)
        push(rnd, CORE_X, 1, sx, sc)
        arrive(rnd, FROM_Y, 0, sy)
        push(rnd, CORE_Y, 0, sy, sc)

    def finish_diagonal(rnd):
        for part in range(2):
            arrive(rnd, DIAGONAL, part, sd)
            push(rnd, CORE_DIAGONAL, part, sd, sc)

    def from_core(rnd, kind, shot):
        for part in range(2):
            arrive(rnd, kind, part, shot)

    def twin(shot):
        return shot + 1 - 2 * c

    def drain(rnd):
        from_core(rnd, CORE_OWN, sc)
        from_core(rnd, CORE_X, twin(sx))
        from_core(rnd, CORE_Y, twin(sy))
        from_core(rnd, CORE_DIAGONAL, twin(sd))

    tile = 256

    def chip_product(column, chip, lanes):
        left = [g[part, chip, pl.ds(s * rows, rows), :] for part in range(2)]
        deep = pl.ds(chip * cols, cols)
        right = [g[part, column, deep, lanes] for part in range(2)]
        dot = functools.partial(jnp.dot, preferred_element_type=jnp.float32)
        real = dot(left[0], right[0]) - dot(left[1], right[1])
        imag = dot(left[0], right[1]) + dot(left[1], right[0])
        return real, imag

    def multiply(rnd, chips, first, last):
        column = order[rnd]

        @pl.loop(0, cols // tile)
        def _(t):
            lanes = pl.ds(pl.multiple_of(t * tile, tile), tile)
            wide = pl.ds(pl.multiple_of(column * cols + t * tile, tile), tile)
            real = imag = None
            for chip in chips:
                a, b = chip_product(column, chip, lanes)
                real = a if real is None else real + a
                imag = b if imag is None else imag + b
            if not first:
                real = real + out_ref[0, 0, :, wide]
                imag = imag + out_ref[0, 1, :, wide]
            out_ref[0, 0, :, wide] = real * scale if last else real
            out_ref[0, 1, :, wide] = imag * scale if last else imag

    every = range(LINE)

    own = pltpu.make_async_copy(x_ref.at[z], g.at[:, z, pl.ds(s * rows, rows), :], own_sem)
    own.start()
    line = [along_line(peer, part) for peer in others for part in range(2)]

    def line_step(i):
        for part in range(2):
            line[2 * i + part].start()

    def line_sent(i):
        for part in range(2):
            line[2 * i + part].wait_send()

    line_step(0)
    send_own(0)
    own.wait()
    relay(0)
    line_sent(0)
    line_step(1)
    for rnd in range(1, LINE):
        for part in range(2):
            line_arrival(order[rnd], part).wait_recv()
        send_own(rnd)
        if rnd < LINE - 1:
            line_sent(rnd)
            if rnd + 1 < LINE - 1:
                line_step(rnd + 1)
        finish_direct(rnd - 1)
        finish_diagonal(rnd - 1)
        if rnd == LINE - 1:
            for done in range(LINE - 2):
                drain(done)
                multiply(done, every, True, True)
        relay(rnd)
    last = LINE - 1
    drain(last - 1)
    multiply(last - 1, every, True, True)
    finish_direct(last)
    from_core(last, CORE_OWN, sc)
    multiply(last, [s // 2], True, False)
    from_core(last, CORE_X, twin(sx))
    multiply(last, [sx // 2], False, False)
    from_core(last, CORE_Y, twin(sy))
    multiply(last, [sy // 2], False, False)
    finish_diagonal(last)
    from_core(last, CORE_DIAGONAL, twin(sd))
    multiply(last, [sd // 2], False, True)
    for copy in started:
        copy.wait_send()


def in_one_kernel(spectra):
    freqs, parts, rows, cols = spectra.shape
    full = cols * LINE
    return pl.pallas_call(
        functools.partial(kernel, rows, cols, -1.0 / math.sqrt(full)),
        out_shape=jax.ShapeDtypeStruct((1, parts, rows, full), jnp.float32),
        in_specs=[pl.BlockSpec(memory_space=pl.ANY)],
        out_specs=pl.BlockSpec(memory_space=pltpu.VMEM),
        scratch_shapes=[
            pltpu.VMEM((parts, LINE, rows * PLANE, cols), jnp.bfloat16),
            pltpu.SemaphoreType.DMA,
            pltpu.SemaphoreType.DMA((LINE, 2)),
            pltpu.SemaphoreType.DMA((LINE, 2)),
            pltpu.SemaphoreType.DMA((LINE, KINDS)),
            pltpu.SemaphoreType.DMA((LINE, KINDS)),
        ],
        compiler_params=pltpu.CompilerParams(
            collective_id=0, has_side_effects=True, vmem_limit_bytes=62 * 2**20
        ),
    )(spectra)


def by_collectives(spectra):
    own_rows = lax.all_to_all(spectra, "rcv", split_axis=0, concat_axis=3, tiled=True)
    full = own_rows.shape[3]
    gathered = lax.all_gather(own_rows, "shot", axis=2, tiled=True)
    dot = functools.partial(jnp.einsum, "ang,agv->anv", preferred_element_type=jnp.float32)
    real = dot(own_rows[:, 0], gathered[:, 0]) - dot(own_rows[:, 1], gathered[:, 1])
    imag = dot(own_rows[:, 0], gathered[:, 1]) + dot(own_rows[:, 1], gathered[:, 0])
    return jnp.stack([real, imag], axis=1) * (-1.0 / math.sqrt(full))


def solution(mesh):
    fits = mesh.shape["shot"] == PLANE and mesh.shape["rcv"] == LINE
    return jax.shard_map(
        in_one_kernel if fits else by_collectives,
        mesh=mesh,
        in_specs=(P(None, None, "shot", "rcv"),),
        out_specs=P("rcv", None, "shot", None),
        check_vma=False,
    )
```

```python
import functools
import math

import jax
import jax.numpy as jnp
from jax import lax
from jax.experimental import pallas as pl
from jax.experimental.pallas import tpu as pltpu
from jax.sharding import PartitionSpec as P

MESH = pl.DeviceIdType.MESH
PLANE = 8
LINE = 4

FROM_X, FROM_Y, DIAGONAL = 0, 2, 4
CORE_OWN, CORE_X, CORE_Y, CORE_DIAGONAL = 6, 8, 10, 12
KINDS = 14


def kernel(rows, cols, scale, x_ref, out_ref, g, acc, own_sem, out_sem, line_send, line_recv, send, recv):
    s, z = lax.axis_index("shot"), lax.axis_index("rcv")
    y, x, c = s // 4, (s // 2) % 2, s % 2
    sx = y * 4 + (1 - x) * 2 + c
    sy = (1 - y) * 4 + x * 2 + c
    sd = (1 - y) * 4 + (1 - x) * 2 + c
    sc = y * 4 + x * 2 + (1 - c)
    half = z // 2
    u = z + half * (3 - 2 * z)

    def mirrored(v):
        return v + half * (3 - 2 * v)

    order = [z, mirrored(1 - u), mirrored(2), mirrored(3)]
    others = order[1:]

    barrier = pltpu.get_barrier_semaphore()
    for peer in (sx, sy, sc):
        pl.semaphore_signal(barrier, inc=1, device_id=(peer, z), device_id_type=MESH)
    for peer in others:
        pl.semaphore_signal(barrier, inc=1, device_id=(s, peer), device_id_type=MESH)
    pl.semaphore_wait(barrier, 6)

    def block(column, part, shot):
        return g.at[part, column, pl.ds(shot * rows, rows), :]

    def along_line(peer, part):
        return pltpu.make_async_remote_copy(
            src_ref=x_ref.at[peer, part],
            dst_ref=block(z, part, s),
            send_sem=line_send.at[peer, part],
            recv_sem=line_recv.at[z, part],
            device_id=(s, peer),
            device_id_type=MESH,
        )

    def line_arrival(source, part):
        return pltpu.make_async_remote_copy(
            src_ref=x_ref.at[source, part],
            dst_ref=block(source, part, s),
            send_sem=line_send.at[source, part],
            recv_sem=line_recv.at[source, part],
            device_id=(s, source),
            device_id_type=MESH,
        )

    started = []

    def push(rnd, kind, part, shot, target, source=None):
        place = block(order[rnd], part, shot)
        copy = pltpu.make_async_remote_copy(
            src_ref=place if source is None else source,
            dst_ref=place,
            send_sem=send.at[rnd, kind + part],
            recv_sem=recv.at[rnd, kind + part],
            device_id=(target, z),
            device_id_type=MESH,
        )
        copy.start()
        started.append(copy)

    def arrive(rnd, kind, part, shot):
        place = block(order[rnd], part, shot)
        pltpu.make_async_remote_copy(
            src_ref=place,
            dst_ref=place,
            send_sem=send.at[rnd, kind + part],
            recv_sem=recv.at[rnd, kind + part],
            device_id=(sx, z),
            device_id_type=MESH,
        ).wait_recv()

    def send_own(rnd):
        for part, kind, target in ((0, FROM_X, sx), (1, FROM_Y, sy), (1, FROM_X, sx), (0, FROM_Y, sy)):
            push(rnd, kind, part, s, target, x_ref.at[z, part] if rnd == 0 else None)
        for part in range(2):
            push(rnd, CORE_OWN, part, s, sc, x_ref.at[z, part] if rnd == 0 else None)

    def relay(rnd):
        arrive(rnd, FROM_X, 0, sx)
        push(rnd, DIAGONAL, 0, sx, sy)
        arrive(rnd, FROM_Y, 1, sy)
        push(rnd, DIAGONAL, 1, sy, sx)
        push(rnd, CORE_X, 0, sx, sc)
        push(rnd, CORE_Y, 1, sy, sc)

    def finish_direct(rnd):
        arrive(rnd, FROM_X, 1, sx)
        push(rnd, CORE_X, 1, sx, sc)
        arrive(rnd, FROM_Y, 0, sy)
        push(rnd, CORE_Y, 0, sy, sc)

    def finish_diagonal(rnd):
        for part in range(2):
            arrive(rnd, DIAGONAL, part, sd)
            push(rnd, CORE_DIAGONAL, part, sd, sc)

    def from_core(rnd, kind, shot):
        for part in range(2):
            arrive(rnd, kind, part, shot)

    def twin(shot):
        return shot + 1 - 2 * c

    def drain(rnd):
        from_core(rnd, CORE_OWN, sc)
        from_core(rnd, CORE_X, twin(sx))
        from_core(rnd, CORE_Y, twin(sy))
        from_core(rnd, CORE_DIAGONAL, twin(sd))

    tile = 256

    def chip_product(column, chip, lanes):
        left = [g[part, chip, pl.ds(s * rows, rows), :] for part in range(2)]
        deep = pl.ds(chip * cols, cols)
        right = [g[part, column, deep, lanes] for part in range(2)]
        dot = functools.partial(jnp.dot, preferred_element_type=jnp.float32)
        real = dot(left[0], right[0]) - dot(left[1], right[1])
        imag = dot(left[0], right[1]) + dot(left[1], right[0])
        return real, imag

    def multiply(rnd, chips, first, last):
        column = order[rnd]

        @pl.loop(0, cols // tile)
        def _(t):
            lanes = pl.ds(pl.multiple_of(t * tile, tile), tile)
            wide = pl.ds(pl.multiple_of(column * cols + t * tile, tile), tile)
            real = imag = None
            for chip in chips:
                a, b = chip_product(column, chip, lanes)
                real = a if real is None else real + a
                imag = b if imag is None else imag + b
            if not first:
                real = real + acc[0, :, wide]
                imag = imag + acc[1, :, wide]
            acc[0, :, wide] = real * scale if last else real
            acc[1, :, wide] = imag * scale if last else imag

    def deliver(rnd):
        lanes = pl.ds(pl.multiple_of(order[rnd] * cols, cols), cols)
        return pltpu.make_async_copy(acc.at[:, :, lanes], out_ref.at[0, :, :, lanes], out_sem.at[rnd])

    every = range(LINE)

    own = pltpu.make_async_copy(x_ref.at[z], g.at[:, z, pl.ds(s * rows, rows), :], own_sem)
    own.start()
    def toward(peer, begin):
        for part in range(2):
            copy = along_line(peer, part)
            copy.start() if begin else copy.wait_send()

    toward(others[0], True)
    send_own(0)

    @pl.when(u == 1)
    def _():
        toward(others[1], True)

    own.wait()
    relay(0)

    @pl.when(u == 1)
    def _():
        toward(others[1], False)
        toward(others[2], True)

    for rnd in range(1, LINE):
        for part in range(2):
            line_arrival(order[rnd], part).wait_recv()
        send_own(rnd)
        finish_direct(rnd - 1)
        finish_diagonal(rnd - 1)
        if rnd < LINE - 1:

            @pl.when(u == 0)
            def _(peer=others[rnd]):
                toward(peer, True)

        if rnd == LINE - 1:
            for done in range(LINE - 2):
                drain(done)
                multiply(done, every, True, True)
                deliver(done).start()
        relay(rnd)
    last = LINE - 1
    drain(last - 1)
    multiply(last - 1, every, True, True)
    deliver(last - 1).start()
    finish_direct(last)
    from_core(last, CORE_OWN, sc)
    multiply(last, [s // 2], True, False)
    from_core(last, CORE_X, twin(sx))
    multiply(last, [sx // 2], False, False)
    from_core(last, CORE_Y, twin(sy))
    multiply(last, [sy // 2], False, False)
    finish_diagonal(last)
    from_core(last, CORE_DIAGONAL, twin(sd))
    multiply(last, [sd // 2], False, True)
    deliver(last).start()
    for rnd in range(LINE):
        deliver(rnd).wait()
    for copy in started:
        copy.wait_send()
    toward(others[0], False)
    toward(others[2], False)

    @pl.when(u == 0)
    def _():
        toward(others[1], False)


def in_one_kernel(spectra):
    freqs, parts, rows, cols = spectra.shape
    full = cols * LINE
    return pl.pallas_call(
        functools.partial(kernel, rows, cols, -1.0 / math.sqrt(full)),
        out_shape=jax.ShapeDtypeStruct((1, parts, rows, full), jnp.float32),
        in_specs=[pl.BlockSpec(memory_space=pltpu.HBM)],
        out_specs=pl.BlockSpec(memory_space=pl.ANY),
        scratch_shapes=[
            pltpu.VMEM((parts, LINE, rows * PLANE, cols), jnp.bfloat16),
            pltpu.VMEM((parts, rows, full), jnp.float32),
            pltpu.SemaphoreType.DMA,
            pltpu.SemaphoreType.DMA((LINE,)),
            pltpu.SemaphoreType.DMA((LINE, 2)),
            pltpu.SemaphoreType.DMA((LINE, 2)),
            pltpu.SemaphoreType.DMA((LINE, KINDS)),
            pltpu.SemaphoreType.DMA((LINE, KINDS)),
        ],
        compiler_params=pltpu.CompilerParams(
            collective_id=0, has_side_effects=True, vmem_limit_bytes=28 * 2**20
        ),
    )(spectra)


def by_collectives(spectra):
    own_rows = lax.all_to_all(spectra, "rcv", split_axis=0, concat_axis=3, tiled=True)
    full = own_rows.shape[3]
    gathered = lax.all_gather(own_rows, "shot", axis=2, tiled=True)
    dot = functools.partial(jnp.einsum, "ang,agv->anv", preferred_element_type=jnp.float32)
    real = dot(own_rows[:, 0], gathered[:, 0]) - dot(own_rows[:, 1], gathered[:, 1])
    imag = dot(own_rows[:, 0], gathered[:, 1]) + dot(own_rows[:, 1], gathered[:, 0])
    return jnp.stack([real, imag], axis=1) * (-1.0 / math.sqrt(full))


def solution(mesh):
    fits = mesh.shape["shot"] == PLANE and mesh.shape["rcv"] == LINE
    return jax.shard_map(
        in_one_kernel if fits else by_collectives,
        mesh=mesh,
        in_specs=(P(None, None, "shot", "rcv"),),
        out_specs=P("rcv", None, "shot", None),
        check_vma=False,
    )
```

```python
import functools
import math

import jax
import jax.numpy as jnp
from jax import lax
from jax.experimental import pallas as pl
from jax.experimental.pallas import tpu as pltpu
from jax.sharding import PartitionSpec as P

MESH = pl.DeviceIdType.MESH
PLANE = 8
LINE = 4

FROM_X, FROM_Y, DIAGONAL = 0, 2, 4
CORE_OWN, CORE_X, CORE_Y, CORE_DIAGONAL = 6, 8, 10, 12
KINDS = 14


def kernel(rows, cols, scale, x_ref, out_ref, g, acc, own_sem, out_sem, line_send, line_recv, send, recv):
    s, z = lax.axis_index("shot"), lax.axis_index("rcv")
    y, x, c = s // 4, (s // 2) % 2, s % 2
    sx = y * 4 + (1 - x) * 2 + c
    sy = (1 - y) * 4 + x * 2 + c
    sd = (1 - y) * 4 + (1 - x) * 2 + c
    sc = y * 4 + x * 2 + (1 - c)
    half = z // 2
    u = z + half * (3 - 2 * z)

    def mirrored(v):
        return v + half * (3 - 2 * v)

    order = [z, mirrored(1 - u), mirrored(2), mirrored(3)]
    others = order[1:]

    barrier = pltpu.get_barrier_semaphore()
    for peer in (sx, sy, sc):
        pl.semaphore_signal(barrier, inc=1, device_id=(peer, z), device_id_type=MESH)
    for peer in others:
        pl.semaphore_signal(barrier, inc=1, device_id=(s, peer), device_id_type=MESH)
    pl.semaphore_wait(barrier, 6)

    def block(column, part, shot):
        return g.at[part, column, pl.ds(shot * rows, rows), :]

    def along_line(peer, part):
        return pltpu.make_async_remote_copy(
            src_ref=x_ref.at[peer, part],
            dst_ref=block(z, part, s),
            send_sem=line_send.at[peer, part],
            recv_sem=line_recv.at[z, part],
            device_id=(s, peer),
            device_id_type=MESH,
        )

    def line_arrival(source, part):
        return pltpu.make_async_remote_copy(
            src_ref=x_ref.at[source, part],
            dst_ref=block(source, part, s),
            send_sem=line_send.at[source, part],
            recv_sem=line_recv.at[source, part],
            device_id=(s, source),
            device_id_type=MESH,
        )

    started = []

    def push(rnd, kind, part, shot, target, source=None):
        place = block(order[rnd], part, shot)
        copy = pltpu.make_async_remote_copy(
            src_ref=place if source is None else source,
            dst_ref=place,
            send_sem=send.at[rnd, kind + part],
            recv_sem=recv.at[rnd, kind + part],
            device_id=(target, z),
            device_id_type=MESH,
        )
        copy.start()
        started.append(copy)

    def arrive(rnd, kind, part, shot):
        place = block(order[rnd], part, shot)
        pltpu.make_async_remote_copy(
            src_ref=place,
            dst_ref=place,
            send_sem=send.at[rnd, kind + part],
            recv_sem=recv.at[rnd, kind + part],
            device_id=(sx, z),
            device_id_type=MESH,
        ).wait_recv()

    def send_relayed(rnd):
        for part, kind, target in ((0, FROM_X, sx), (1, FROM_Y, sy), (0, CORE_OWN, sc), (1, CORE_OWN, sc)):
            push(rnd, kind, part, s, target, x_ref.at[z, part] if rnd == 0 else None)

    def send_direct(rnd):
        for part, kind, target in ((1, FROM_X, sx), (0, FROM_Y, sy)):
            push(rnd, kind, part, s, target, x_ref.at[z, part] if rnd == 0 else None)

    def relay(rnd):
        arrive(rnd, FROM_X, 0, sx)
        push(rnd, DIAGONAL, 0, sx, sy)
        arrive(rnd, FROM_Y, 1, sy)
        push(rnd, DIAGONAL, 1, sy, sx)
        push(rnd, CORE_X, 0, sx, sc)
        push(rnd, CORE_Y, 1, sy, sc)

    def finish_direct(rnd):
        arrive(rnd, FROM_X, 1, sx)
        push(rnd, CORE_X, 1, sx, sc)
        arrive(rnd, FROM_Y, 0, sy)
        push(rnd, CORE_Y, 0, sy, sc)

    def finish_diagonal(rnd):
        for part in range(2):
            arrive(rnd, DIAGONAL, part, sd)
            push(rnd, CORE_DIAGONAL, part, sd, sc)

    def from_core(rnd, kind, shot):
        for part in range(2):
            arrive(rnd, kind, part, shot)

    def twin(shot):
        return shot + 1 - 2 * c

    def drain(rnd):
        from_core(rnd, CORE_OWN, sc)
        from_core(rnd, CORE_X, twin(sx))
        from_core(rnd, CORE_Y, twin(sy))
        from_core(rnd, CORE_DIAGONAL, twin(sd))

    tile = 256

    def chip_product(column, chip, lanes):
        left = [g[part, chip, pl.ds(s * rows, rows), :] for part in range(2)]
        deep = pl.ds(chip * cols, cols)
        right = [g[part, column, deep, lanes] for part in range(2)]
        dot = functools.partial(jnp.dot, preferred_element_type=jnp.float32)
        real = dot(left[0], right[0]) - dot(left[1], right[1])
        imag = dot(left[0], right[1]) + dot(left[1], right[0])
        return real, imag

    def multiply(rnd, chips, first, last):
        column = order[rnd]

        @pl.loop(0, cols // tile)
        def _(t):
            lanes = pl.ds(pl.multiple_of(t * tile, tile), tile)
            wide = pl.ds(pl.multiple_of(column * cols + t * tile, tile), tile)
            real = imag = None
            for chip in chips:
                a, b = chip_product(column, chip, lanes)
                real = a if real is None else real + a
                imag = b if imag is None else imag + b
            if not first:
                real = real + acc[0, :, wide]
                imag = imag + acc[1, :, wide]
            acc[0, :, wide] = real * scale if last else real
            acc[1, :, wide] = imag * scale if last else imag

    def multiply_part(part, chip, last, first=0, deep=cols):
        column = order[-1]

        @pl.loop(0, cols // tile)
        def _(t):
            lanes = pl.ds(pl.multiple_of(t * tile, tile), tile)
            wide = pl.ds(pl.multiple_of(column * cols + t * tile, tile), tile)
            if deep == cols:
                left = [g[p, chip, pl.ds(s * rows, rows), :] for p in range(2)]
            else:
                span = pl.ds(pl.multiple_of(first, rows), rows)
                left = [g[p, chip, pl.ds(s * rows, rows), span] for p in range(2)]
            right = g[part, column, pl.ds(chip * cols + first, deep), lanes]
            dot = functools.partial(jnp.dot, preferred_element_type=jnp.float32)
            a, b = dot(left[part], right), dot(left[1 - part], right)
            real = acc[0, :, wide] + (a if part == 0 else -a)
            imag = acc[1, :, wide] + b
            acc[0, :, wide] = real * scale if last else real
            acc[1, :, wide] = imag * scale if last else imag

    def multiply_shot(part, shot, last):
        multiply_part(part, shot // 2, last, (shot % 2) * rows, rows)

    def deliver(rnd):
        lanes = pl.ds(pl.multiple_of(order[rnd] * cols, cols), cols)
        return pltpu.make_async_copy(acc.at[:, :, lanes], out_ref.at[0, :, :, lanes], out_sem.at[rnd])

    every = range(LINE)

    own = pltpu.make_async_copy(x_ref.at[z], g.at[:, z, pl.ds(s * rows, rows), :], own_sem)
    own.start()
    def toward(peer, begin):
        for part in range(2):
            copy = along_line(peer, part)
            copy.start() if begin else copy.wait_send()

    toward(others[0], True)
    send_relayed(0)
    send_direct(0)

    @pl.when(u == 1)
    def _():
        toward(others[1], True)

    own.wait()
    relay(0)

    @pl.when(u == 1)
    def _():
        toward(others[1], False)
        toward(others[2], True)

    for rnd in range(1, LINE):
        for part in range(2):
            line_arrival(order[rnd], part).wait_recv()
        send_relayed(rnd)
        finish_direct(rnd - 1)
        if rnd == LINE - 1:
            drain(0)
            multiply(0, every, True, True)
            deliver(0).start()
        finish_diagonal(rnd - 1)
        send_direct(rnd)
        if rnd < LINE - 1:

            @pl.when(u == 0)
            def _(peer=others[rnd]):
                toward(peer, True)

        if rnd == LINE - 1:
            drain(1)
            multiply(1, every, True, True)
            deliver(1).start()
        relay(rnd)
    last = LINE - 1
    drain(last - 1)
    multiply(last - 1, every, True, True)
    deliver(last - 1).start()
    from_core(last, CORE_OWN, sc)
    multiply(last, [s // 2], True, False)
    finish_direct(last)
    arrive(last, CORE_X, 0, twin(sx))
    multiply_part(0, sx // 2, False)
    arrive(last, CORE_Y, 1, twin(sy))
    multiply_part(1, sy // 2, False)
    arrive(last, CORE_X, 1, twin(sx))
    multiply_part(1, sx // 2, False)
    arrive(last, CORE_Y, 0, twin(sy))
    multiply_part(0, sy // 2, False)
    finish_diagonal(last)
    for part in range(2):
        multiply_shot(part, sd, False)
    for part in range(2):
        arrive(last, CORE_DIAGONAL, part, twin(sd))
        multiply_shot(part, twin(sd), part == 1)
    deliver(last).start()
    for rnd in range(LINE):
        deliver(rnd).wait()
    for copy in started:
        copy.wait_send()
    toward(others[0], False)
    toward(others[2], False)

    @pl.when(u == 0)
    def _():
        toward(others[1], False)


def in_one_kernel(spectra):
    freqs, parts, rows, cols = spectra.shape
    full = cols * LINE
    return pl.pallas_call(
        functools.partial(kernel, rows, cols, -1.0 / math.sqrt(full)),
        out_shape=jax.ShapeDtypeStruct((1, parts, rows, full), jnp.float32),
        in_specs=[pl.BlockSpec(memory_space=pltpu.HBM)],
        out_specs=pl.BlockSpec(memory_space=pl.ANY),
        scratch_shapes=[
            pltpu.VMEM((parts, LINE, rows * PLANE, cols), jnp.bfloat16),
            pltpu.VMEM((parts, rows, full), jnp.float32),
            pltpu.SemaphoreType.DMA,
            pltpu.SemaphoreType.DMA((LINE,)),
            pltpu.SemaphoreType.DMA((LINE, 2)),
            pltpu.SemaphoreType.DMA((LINE, 2)),
            pltpu.SemaphoreType.DMA((LINE, KINDS)),
            pltpu.SemaphoreType.DMA((LINE, KINDS)),
        ],
        compiler_params=pltpu.CompilerParams(
            collective_id=0, has_side_effects=True, vmem_limit_bytes=28 * 2**20
        ),
    )(pltpu.with_memory_space_constraint(spectra, pltpu.HBM))


def by_collectives(spectra):
    own_rows = lax.all_to_all(spectra, "rcv", split_axis=0, concat_axis=3, tiled=True)
    full = own_rows.shape[3]
    gathered = lax.all_gather(own_rows, "shot", axis=2, tiled=True)
    dot = functools.partial(jnp.einsum, "ang,agv->anv", preferred_element_type=jnp.float32)
    real = dot(own_rows[:, 0], gathered[:, 0]) - dot(own_rows[:, 1], gathered[:, 1])
    imag = dot(own_rows[:, 0], gathered[:, 1]) + dot(own_rows[:, 1], gathered[:, 0])
    return jnp.stack([real, imag], axis=1) * (-1.0 / math.sqrt(full))


def solution(mesh):
    fits = mesh.shape["shot"] == PLANE and mesh.shape["rcv"] == LINE
    return jax.shard_map(
        in_one_kernel if fits else by_collectives,
        mesh=mesh,
        in_specs=(P(None, None, "shot", "rcv"),),
        out_specs=P("rcv", None, "shot", None),
        check_vma=False,
    )
```

```python
import functools
import math

import jax
import jax.numpy as jnp
from jax import lax
from jax.experimental import pallas as pl
from jax.experimental.pallas import tpu as pltpu
from jax.sharding import PartitionSpec as P

MESH = pl.DeviceIdType.MESH
PLANE = 8
LINE = 4

FROM_X, FROM_Y, DIAGONAL = 0, 2, 4
CORE_OWN, CORE_X, CORE_Y, CORE_DIAGONAL = 6, 8, 10, 12
KINDS = 14


def kernel(rows, cols, scale, x_ref, out_ref, g, acc, own_sem, out_sem, line_send, line_recv, send, recv):
    s, z = lax.axis_index("shot"), lax.axis_index("rcv")
    y, x, c = s // 4, (s // 2) % 2, s % 2
    sx = y * 4 + (1 - x) * 2 + c
    sy = (1 - y) * 4 + x * 2 + c
    sd = (1 - y) * 4 + (1 - x) * 2 + c
    sc = y * 4 + x * 2 + (1 - c)
    half = z // 2
    u = z + half * (3 - 2 * z)

    def mirrored(v):
        return v + half * (3 - 2 * v)

    order = [z, mirrored(1 - u), mirrored(2), mirrored(3)]
    others = order[1:]

    barrier = pltpu.get_barrier_semaphore()
    for peer in (sx, sy, sc):
        pl.semaphore_signal(barrier, inc=1, device_id=(peer, z), device_id_type=MESH)
    for peer in others:
        pl.semaphore_signal(barrier, inc=1, device_id=(s, peer), device_id_type=MESH)
    pl.semaphore_wait(barrier, 6)

    def block(column, part, shot):
        return g.at[part, column, pl.ds(shot * rows, rows), :]

    def along_line(peer, part):
        return pltpu.make_async_remote_copy(
            src_ref=x_ref.at[peer, part],
            dst_ref=block(z, part, s),
            send_sem=line_send.at[peer, part],
            recv_sem=line_recv.at[z, part],
            device_id=(s, peer),
            device_id_type=MESH,
        )

    def line_arrival(source, part):
        return pltpu.make_async_remote_copy(
            src_ref=x_ref.at[source, part],
            dst_ref=block(source, part, s),
            send_sem=line_send.at[source, part],
            recv_sem=line_recv.at[source, part],
            device_id=(s, source),
            device_id_type=MESH,
        )

    started = []

    def push(rnd, kind, part, shot, target, source=None):
        place = block(order[rnd], part, shot)
        copy = pltpu.make_async_remote_copy(
            src_ref=place if source is None else source,
            dst_ref=place,
            send_sem=send.at[rnd, kind + part],
            recv_sem=recv.at[rnd, kind + part],
            device_id=(target, z),
            device_id_type=MESH,
        )
        copy.start()
        started.append(copy)

    def arrive(rnd, kind, part, shot):
        place = block(order[rnd], part, shot)
        pltpu.make_async_remote_copy(
            src_ref=place,
            dst_ref=place,
            send_sem=send.at[rnd, kind + part],
            recv_sem=recv.at[rnd, kind + part],
            device_id=(sx, z),
            device_id_type=MESH,
        ).wait_recv()

    def send_relayed(rnd):
        for part, kind, target in ((0, FROM_X, sx), (1, FROM_Y, sy), (0, CORE_OWN, sc), (1, CORE_OWN, sc)):
            push(rnd, kind, part, s, target, x_ref.at[z, part] if rnd == 0 else None)

    def send_direct(rnd):
        for part, kind, target in ((1, FROM_X, sx), (0, FROM_Y, sy)):
            push(rnd, kind, part, s, target, x_ref.at[z, part] if rnd == 0 else None)

    def relay(rnd):
        arrive(rnd, FROM_X, 0, sx)
        push(rnd, DIAGONAL, 0, sx, sy)
        arrive(rnd, FROM_Y, 1, sy)
        push(rnd, DIAGONAL, 1, sy, sx)
        push(rnd, CORE_X, 0, sx, sc)
        push(rnd, CORE_Y, 1, sy, sc)

    def finish_direct(rnd):
        arrive(rnd, FROM_X, 1, sx)
        push(rnd, CORE_X, 1, sx, sc)
        arrive(rnd, FROM_Y, 0, sy)
        push(rnd, CORE_Y, 0, sy, sc)

    def finish_diagonal(rnd):
        for part in range(2):
            arrive(rnd, DIAGONAL, part, sd)
            push(rnd, CORE_DIAGONAL, part, sd, sc)

    def from_core(rnd, kind, shot):
        for part in range(2):
            arrive(rnd, kind, part, shot)

    def twin(shot):
        return shot + 1 - 2 * c

    def drain(rnd):
        from_core(rnd, CORE_OWN, sc)
        from_core(rnd, CORE_X, twin(sx))
        from_core(rnd, CORE_Y, twin(sy))
        from_core(rnd, CORE_DIAGONAL, twin(sd))

    tile = 512

    def chip_product(column, chip, lanes):
        left = [g[part, chip, pl.ds(s * rows, rows), :] for part in range(2)]
        deep = pl.ds(chip * cols, cols)
        right = [g[part, column, deep, lanes] for part in range(2)]
        dot = functools.partial(jnp.dot, preferred_element_type=jnp.float32)
        real = dot(left[0], right[0]) - dot(left[1], right[1])
        imag = dot(left[0], right[1]) + dot(left[1], right[0])
        return real, imag

    def multiply(rnd, chips, first, last):
        column = order[rnd]

        @pl.loop(0, cols // tile)
        def _(t):
            lanes = pl.ds(pl.multiple_of(t * tile, tile), tile)
            wide = pl.ds(pl.multiple_of(column * cols + t * tile, tile), tile)
            real = imag = None
            for chip in chips:
                a, b = chip_product(column, chip, lanes)
                real = a if real is None else real + a
                imag = b if imag is None else imag + b
            if not first:
                real = real + acc[0, :, wide]
                imag = imag + acc[1, :, wide]
            acc[0, :, wide] = real * scale if last else real
            acc[1, :, wide] = imag * scale if last else imag

    def multiply_part(part, chip, last, first=0, deep=cols):
        column = order[-1]

        @pl.loop(0, cols // tile)
        def _(t):
            lanes = pl.ds(pl.multiple_of(t * tile, tile), tile)
            wide = pl.ds(pl.multiple_of(column * cols + t * tile, tile), tile)
            if deep == cols:
                left = [g[p, chip, pl.ds(s * rows, rows), :] for p in range(2)]
            else:
                span = pl.ds(pl.multiple_of(first, rows), rows)
                left = [g[p, chip, pl.ds(s * rows, rows), span] for p in range(2)]
            right = g[part, column, pl.ds(chip * cols + first, deep), lanes]
            dot = functools.partial(jnp.dot, preferred_element_type=jnp.float32)
            a, b = dot(left[part], right), dot(left[1 - part], right)
            real = acc[0, :, wide] + (a if part == 0 else -a)
            imag = acc[1, :, wide] + b
            acc[0, :, wide] = real * scale if last else real
            acc[1, :, wide] = imag * scale if last else imag

    def multiply_shot(part, shot, last):
        multiply_part(part, shot // 2, last, (shot % 2) * rows, rows)

    def deliver(rnd):
        lanes = pl.ds(pl.multiple_of(order[rnd] * cols, cols), cols)
        return pltpu.make_async_copy(acc.at[:, :, lanes], out_ref.at[0, :, :, lanes], out_sem.at[rnd])

    every = range(LINE)

    own = pltpu.make_async_copy(x_ref.at[z], g.at[:, z, pl.ds(s * rows, rows), :], own_sem)
    own.start()
    def toward(peer, begin):
        for part in range(2):
            copy = along_line(peer, part)
            copy.start() if begin else copy.wait_send()

    toward(others[0], True)
    send_relayed(0)
    send_direct(0)

    @pl.when(u == 1)
    def _():
        toward(others[1], True)

    own.wait()
    relay(0)

    @pl.when(u == 1)
    def _():
        toward(others[1], False)
        toward(others[2], True)

    for rnd in range(1, LINE):
        for part in range(2):
            line_arrival(order[rnd], part).wait_recv()
        send_relayed(rnd)
        finish_direct(rnd - 1)
        if rnd == LINE - 1:
            drain(0)
            multiply(0, every, True, True)
            deliver(0).start()
        if rnd == LINE - 1:
            send_direct(rnd)
        finish_diagonal(rnd - 1)
        if rnd < LINE - 1:
            send_direct(rnd)
        if rnd < LINE - 1:

            @pl.when(u == 0)
            def _(peer=others[rnd]):
                toward(peer, True)

        if rnd == LINE - 1:
            drain(1)
            multiply(1, every, True, True)
            deliver(1).start()
        relay(rnd)
    last = LINE - 1
    drain(last - 1)
    multiply(last - 1, every, True, True)
    deliver(last - 1).start()
    from_core(last, CORE_OWN, sc)
    multiply(last, [s // 2], True, False)
    finish_direct(last)
    arrive(last, CORE_X, 0, twin(sx))
    multiply_part(0, sx // 2, False)
    arrive(last, CORE_Y, 1, twin(sy))
    multiply_part(1, sy // 2, False)
    arrive(last, CORE_X, 1, twin(sx))
    multiply_part(1, sx // 2, False)
    arrive(last, CORE_Y, 0, twin(sy))
    multiply_part(0, sy // 2, False)
    finish_diagonal(last)
    for part in range(2):
        multiply_shot(part, sd, False)
    for part in range(2):
        arrive(last, CORE_DIAGONAL, part, twin(sd))
        multiply_shot(part, twin(sd), part == 1)
    deliver(last).start()
    for rnd in range(LINE):
        deliver(rnd).wait()
    for copy in started:
        copy.wait_send()
    toward(others[0], False)
    toward(others[2], False)

    @pl.when(u == 0)
    def _():
        toward(others[1], False)


def in_one_kernel(spectra):
    freqs, parts, rows, cols = spectra.shape
    full = cols * LINE
    return pl.pallas_call(
        functools.partial(kernel, rows, cols, -1.0 / math.sqrt(full)),
        out_shape=jax.ShapeDtypeStruct((1, parts, rows, full), jnp.float32),
        in_specs=[pl.BlockSpec(memory_space=pltpu.HBM)],
        out_specs=pl.BlockSpec(memory_space=pl.ANY),
        scratch_shapes=[
            pltpu.VMEM((parts, LINE, rows * PLANE, cols), jnp.bfloat16),
            pltpu.VMEM((parts, rows, full), jnp.float32),
            pltpu.SemaphoreType.DMA,
            pltpu.SemaphoreType.DMA((LINE,)),
            pltpu.SemaphoreType.DMA((LINE, 2)),
            pltpu.SemaphoreType.DMA((LINE, 2)),
            pltpu.SemaphoreType.DMA((LINE, KINDS)),
            pltpu.SemaphoreType.DMA((LINE, KINDS)),
        ],
        compiler_params=pltpu.CompilerParams(
            collective_id=0, has_side_effects=True, vmem_limit_bytes=28 * 2**20
        ),
    )(pltpu.with_memory_space_constraint(spectra, pltpu.HBM))


def by_collectives(spectra):
    own_rows = lax.all_to_all(spectra, "rcv", split_axis=0, concat_axis=3, tiled=True)
    full = own_rows.shape[3]
    gathered = lax.all_gather(own_rows, "shot", axis=2, tiled=True)
    dot = functools.partial(jnp.einsum, "ang,agv->anv", preferred_element_type=jnp.float32)
    real = dot(own_rows[:, 0], gathered[:, 0]) - dot(own_rows[:, 1], gathered[:, 1])
    imag = dot(own_rows[:, 0], gathered[:, 1]) + dot(own_rows[:, 1], gathered[:, 0])
    return jnp.stack([real, imag], axis=1) * (-1.0 / math.sqrt(full))


def solution(mesh):
    fits = mesh.shape["shot"] == PLANE and mesh.shape["rcv"] == LINE
    return jax.shard_map(
        in_one_kernel if fits else by_collectives,
        mesh=mesh,
        in_specs=(P(None, None, "shot", "rcv"),),
        out_specs=P("rcv", None, "shot", None),
        check_vma=False,
    )
```

```python
import functools
import math

import jax
import jax.numpy as jnp
from jax import lax
from jax.experimental import pallas as pl
from jax.experimental.pallas import tpu as pltpu
from jax.sharding import PartitionSpec as P

MESH = pl.DeviceIdType.MESH
PLANE = 8
LINE = 4

FROM_X, FROM_Y, DIAGONAL = 0, 2, 4
CORE_OWN, CORE_X, CORE_Y, CORE_DIAGONAL = 6, 8, 10, 12
KINDS = 14


def kernel(rows, cols, scale, x_ref, out_ref, g, acc, own_sem, out_sem, line_send, line_recv, send, recv):
    s, z = lax.axis_index("shot"), lax.axis_index("rcv")
    y, x, c = s // 4, (s // 2) % 2, s % 2
    sx = y * 4 + (1 - x) * 2 + c
    sy = (1 - y) * 4 + x * 2 + c
    sd = (1 - y) * 4 + (1 - x) * 2 + c
    sc = y * 4 + x * 2 + (1 - c)
    half = z // 2
    u = z + half * (3 - 2 * z)

    def mirrored(v):
        return v + half * (3 - 2 * v)

    order = [z, mirrored(1 - u), mirrored(2), mirrored(3)]
    others = order[1:]

    barrier = pltpu.get_barrier_semaphore()
    for peer in (sx, sy, sc):
        pl.semaphore_signal(barrier, inc=1, device_id=(peer, z), device_id_type=MESH)
    for peer in others:
        pl.semaphore_signal(barrier, inc=1, device_id=(s, peer), device_id_type=MESH)
    pl.semaphore_wait(barrier, 6)

    def block(column, part, shot):
        return g.at[part, column, pl.ds(shot * rows, rows), :]

    def along_line(peer, part):
        return pltpu.make_async_remote_copy(
            src_ref=x_ref.at[peer, part],
            dst_ref=block(z, part, s),
            send_sem=line_send.at[peer, part],
            recv_sem=line_recv.at[z, part],
            device_id=(s, peer),
            device_id_type=MESH,
        )

    def line_arrival(source, part):
        return pltpu.make_async_remote_copy(
            src_ref=x_ref.at[source, part],
            dst_ref=block(source, part, s),
            send_sem=line_send.at[source, part],
            recv_sem=line_recv.at[source, part],
            device_id=(s, source),
            device_id_type=MESH,
        )

    started = []

    def push(rnd, kind, part, shot, target, source=None):
        place = block(order[rnd], part, shot)
        copy = pltpu.make_async_remote_copy(
            src_ref=place if source is None else source,
            dst_ref=place,
            send_sem=send.at[rnd, kind + part],
            recv_sem=recv.at[rnd, kind + part],
            device_id=(target, z),
            device_id_type=MESH,
        )
        copy.start()
        started.append(copy)

    def arrive(rnd, kind, part, shot):
        place = block(order[rnd], part, shot)
        pltpu.make_async_remote_copy(
            src_ref=place,
            dst_ref=place,
            send_sem=send.at[rnd, kind + part],
            recv_sem=recv.at[rnd, kind + part],
            device_id=(sx, z),
            device_id_type=MESH,
        ).wait_recv()

    def send_relayed(rnd):
        for part, kind, target in ((0, FROM_X, sx), (1, FROM_Y, sy), (0, CORE_OWN, sc), (1, CORE_OWN, sc)):
            push(rnd, kind, part, s, target, x_ref.at[z, part] if rnd == 0 else None)

    def send_direct(rnd):
        for part, kind, target in ((1, FROM_X, sx), (0, FROM_Y, sy)):
            push(rnd, kind, part, s, target, x_ref.at[z, part] if rnd == 0 else None)

    def relay(rnd):
        arrive(rnd, FROM_X, 0, sx)
        push(rnd, DIAGONAL, 0, sx, sy)
        arrive(rnd, FROM_Y, 1, sy)
        push(rnd, DIAGONAL, 1, sy, sx)
        push(rnd, CORE_X, 0, sx, sc)
        push(rnd, CORE_Y, 1, sy, sc)

    def finish_direct(rnd):
        arrive(rnd, FROM_X, 1, sx)
        push(rnd, CORE_X, 1, sx, sc)
        arrive(rnd, FROM_Y, 0, sy)
        push(rnd, CORE_Y, 0, sy, sc)

    def finish_diagonal(rnd):
        for part in range(2):
            arrive(rnd, DIAGONAL, part, sd)
            push(rnd, CORE_DIAGONAL, part, sd, sc)

    def from_core(rnd, kind, shot):
        for part in range(2):
            arrive(rnd, kind, part, shot)

    def twin(shot):
        return shot + 1 - 2 * c

    def drain(rnd):
        from_core(rnd, CORE_OWN, sc)
        from_core(rnd, CORE_X, twin(sx))
        from_core(rnd, CORE_Y, twin(sy))
        from_core(rnd, CORE_DIAGONAL, twin(sd))

    tile = 512

    def chip_product(column, chip, lanes):
        left = [g[part, chip, pl.ds(s * rows, rows), :] for part in range(2)]
        deep = pl.ds(chip * cols, cols)
        right = [g[part, column, deep, lanes] for part in range(2)]
        dot = functools.partial(jnp.dot, preferred_element_type=jnp.float32)
        real = dot(left[0], right[0]) - dot(left[1], right[1])
        imag = dot(left[0], right[1]) + dot(left[1], right[0])
        return real, imag

    def multiply(rnd, chips, first, last):
        column = order[rnd]

        @pl.loop(0, cols // tile)
        def _(t):
            lanes = pl.ds(pl.multiple_of(t * tile, tile), tile)
            wide = pl.ds(pl.multiple_of(column * cols + t * tile, tile), tile)
            real = imag = None
            for chip in chips:
                a, b = chip_product(column, chip, lanes)
                real = a if real is None else real + a
                imag = b if imag is None else imag + b
            if not first:
                real = real + acc[0, :, wide]
                imag = imag + acc[1, :, wide]
            acc[0, :, wide] = real * scale if last else real
            acc[1, :, wide] = imag * scale if last else imag

    def multiply_part(part, chip, last, first=0, deep=cols):
        column = order[-1]

        @pl.loop(0, cols // tile)
        def _(t):
            lanes = pl.ds(pl.multiple_of(t * tile, tile), tile)
            wide = pl.ds(pl.multiple_of(column * cols + t * tile, tile), tile)
            if deep == cols:
                left = [g[p, chip, pl.ds(s * rows, rows), :] for p in range(2)]
            else:
                span = pl.ds(pl.multiple_of(first, rows), rows)
                left = [g[p, chip, pl.ds(s * rows, rows), span] for p in range(2)]
            right = g[part, column, pl.ds(chip * cols + first, deep), lanes]
            dot = functools.partial(jnp.dot, preferred_element_type=jnp.float32)
            a, b = dot(left[part], right), dot(left[1 - part], right)
            real = acc[0, :, wide] + (a if part == 0 else -a)
            imag = acc[1, :, wide] + b
            acc[0, :, wide] = real * scale if last else real
            acc[1, :, wide] = imag * scale if last else imag

    def multiply_shot(part, shot, last):
        multiply_part(part, shot // 2, last, (shot % 2) * rows, rows)

    def deliver(rnd):
        lanes = pl.ds(pl.multiple_of(order[rnd] * cols, cols), cols)
        return pltpu.make_async_copy(acc.at[:, :, lanes], out_ref.at[0, :, :, lanes], out_sem.at[rnd])

    every = range(LINE)

    own = pltpu.make_async_copy(x_ref.at[z], g.at[:, z, pl.ds(s * rows, rows), :], own_sem)
    own.start()
    def toward(peer, begin):
        for part in range(2):
            copy = along_line(peer, part)
            copy.start() if begin else copy.wait_send()

    toward(others[0], True)
    send_relayed(0)
    send_direct(0)

    @pl.when(u == 1)
    def _():
        toward(others[1], True)

    own.wait()
    relay(0)

    @pl.when(u == 1)
    def _():
        toward(others[1], False)
        toward(others[2], True)

    for rnd in range(1, LINE):
        for part in range(2):
            line_arrival(order[rnd], part).wait_recv()
        send_relayed(rnd)
        finish_direct(rnd - 1)
        if rnd == LINE - 1:
            drain(0)
            multiply(0, every, True, True)
            deliver(0).start()
        finish_diagonal(rnd - 1)
        send_direct(rnd)
        if rnd < LINE - 1:

            @pl.when(u == 0)
            def _(peer=others[rnd]):
                toward(peer, True)

        if rnd == LINE - 1:
            drain(1)
            multiply(1, every, True, True)
            deliver(1).start()
        relay(rnd)
    last = LINE - 1
    drain(last - 1)
    multiply(last - 1, every, True, True)
    deliver(last - 1).start()
    from_core(last, CORE_OWN, sc)
    multiply(last, [s // 2], True, False)
    finish_direct(last)
    arrive(last, CORE_X, 0, twin(sx))
    multiply_part(0, sx // 2, False)
    arrive(last, CORE_Y, 1, twin(sy))
    multiply_part(1, sy // 2, False)
    arrive(last, CORE_X, 1, twin(sx))
    multiply_part(1, sx // 2, False)
    arrive(last, CORE_Y, 0, twin(sy))
    multiply_part(0, sy // 2, False)
    finish_diagonal(last)
    for part in range(2):
        multiply_shot(part, sd, False)
    for part in range(2):
        arrive(last, CORE_DIAGONAL, part, twin(sd))
        multiply_shot(part, twin(sd), part == 1)
    deliver(last).start()
    for rnd in range(LINE):
        deliver(rnd).wait()
    for copy in started:
        copy.wait_send()
    toward(others[0], False)
    toward(others[2], False)

    @pl.when(u == 0)
    def _():
        toward(others[1], False)


def in_one_kernel(spectra):
    freqs, parts, rows, cols = spectra.shape
    full = cols * LINE
    return pl.pallas_call(
        functools.partial(kernel, rows, cols, -1.0 / math.sqrt(full)),
        out_shape=jax.ShapeDtypeStruct((1, parts, rows, full), jnp.float32),
        in_specs=[pl.BlockSpec(memory_space=pltpu.HBM)],
        out_specs=pl.BlockSpec(memory_space=pl.ANY),
        scratch_shapes=[
            pltpu.VMEM((parts, LINE, rows * PLANE, cols), jnp.bfloat16),
            pltpu.VMEM((parts, rows, full), jnp.float32),
            pltpu.SemaphoreType.DMA,
            pltpu.SemaphoreType.DMA((LINE,)),
            pltpu.SemaphoreType.DMA((LINE, 2)),
            pltpu.SemaphoreType.DMA((LINE, 2)),
            pltpu.SemaphoreType.DMA((LINE, KINDS)),
            pltpu.SemaphoreType.DMA((LINE, KINDS)),
        ],
        compiler_params=pltpu.CompilerParams(
            collective_id=0, has_side_effects=True, vmem_limit_bytes=28 * 2**20
        ),
    )(pltpu.with_memory_space_constraint(spectra, pltpu.HBM))


def by_collectives(spectra):
    own_rows = lax.all_to_all(spectra, "rcv", split_axis=0, concat_axis=3, tiled=True)
    full = own_rows.shape[3]
    gathered = lax.all_gather(own_rows, "shot", axis=2, tiled=True)
    dot = functools.partial(jnp.einsum, "ang,agv->anv", preferred_element_type=jnp.float32)
    real = dot(own_rows[:, 0], gathered[:, 0]) - dot(own_rows[:, 1], gathered[:, 1])
    imag = dot(own_rows[:, 0], gathered[:, 1]) + dot(own_rows[:, 1], gathered[:, 0])
    return jnp.stack([real, imag], axis=1) * (-1.0 / math.sqrt(full))


def solution(mesh):
    fits = mesh.shape["shot"] == PLANE and mesh.shape["rcv"] == LINE
    return jax.shard_map(
        in_one_kernel if fits else by_collectives,
        mesh=mesh,
        in_specs=(P(None, None, "shot", "rcv"),),
        out_specs=P("rcv", None, "shot", None),
        check_vma=False,
    )
```

```python
import functools
import math

import jax
import jax.numpy as jnp
from jax import lax
from jax.experimental import pallas as pl
from jax.experimental.pallas import tpu as pltpu
from jax.sharding import PartitionSpec as P

MESH = pl.DeviceIdType.MESH
PLANE = 8
LINE = 4

FROM_X, FROM_Y, DIAGONAL = 0, 2, 4
CORE_OWN, CORE_X, CORE_Y, CORE_DIAGONAL = 6, 8, 10, 12
KINDS = 14


def kernel(rows, cols, scale, x_ref, out_ref, g, acc, own_sem, out_sem, line_send, line_recv, send, recv):
    s, z = lax.axis_index("shot"), lax.axis_index("rcv")
    y, x, c = s // 4, (s // 2) % 2, s % 2
    sx = y * 4 + (1 - x) * 2 + c
    sy = (1 - y) * 4 + x * 2 + c
    sd = (1 - y) * 4 + (1 - x) * 2 + c
    sc = y * 4 + x * 2 + (1 - c)
    half = z // 2
    u = z + half * (3 - 2 * z)

    def mirrored(v):
        return v + half * (3 - 2 * v)

    order = [z, mirrored(1 - u), mirrored(2), mirrored(3)]
    others = order[1:]

    barrier = pltpu.get_barrier_semaphore()
    for peer in (sx, sy, sc):
        pl.semaphore_signal(barrier, inc=1, device_id=(peer, z), device_id_type=MESH)
    for peer in others:
        pl.semaphore_signal(barrier, inc=1, device_id=(s, peer), device_id_type=MESH)
    pl.semaphore_wait(barrier, 6)

    def block(column, part, shot):
        return g.at[part, column, pl.ds(shot * rows, rows), :]

    def along_line(peer, part):
        return pltpu.make_async_remote_copy(
            src_ref=x_ref.at[peer, part],
            dst_ref=block(z, part, s),
            send_sem=line_send.at[peer, part],
            recv_sem=line_recv.at[z, part],
            device_id=(s, peer),
            device_id_type=MESH,
        )

    def line_arrival(source, part):
        return pltpu.make_async_remote_copy(
            src_ref=x_ref.at[source, part],
            dst_ref=block(source, part, s),
            send_sem=line_send.at[source, part],
            recv_sem=line_recv.at[source, part],
            device_id=(s, source),
            device_id_type=MESH,
        )

    started = []

    def push(rnd, kind, part, shot, target, source=None):
        place = block(order[rnd], part, shot)
        copy = pltpu.make_async_remote_copy(
            src_ref=place if source is None else source,
            dst_ref=place,
            send_sem=send.at[rnd, kind + part],
            recv_sem=recv.at[rnd, kind + part],
            device_id=(target, z),
            device_id_type=MESH,
        )
        copy.start()
        started.append(copy)

    def arrive(rnd, kind, part, shot):
        place = block(order[rnd], part, shot)
        pltpu.make_async_remote_copy(
            src_ref=place,
            dst_ref=place,
            send_sem=send.at[rnd, kind + part],
            recv_sem=recv.at[rnd, kind + part],
            device_id=(sx, z),
            device_id_type=MESH,
        ).wait_recv()

    def send_relayed(rnd):
        for part, kind, target in ((0, FROM_X, sx), (1, FROM_Y, sy), (0, CORE_OWN, sc), (1, CORE_OWN, sc)):
            push(rnd, kind, part, s, target, x_ref.at[z, part] if rnd == 0 else None)

    def send_direct(rnd):
        for part, kind, target in ((1, FROM_X, sx), (0, FROM_Y, sy)):
            push(rnd, kind, part, s, target, x_ref.at[z, part] if rnd == 0 else None)

    def relay(rnd):
        arrive(rnd, FROM_X, 0, sx)
        push(rnd, DIAGONAL, 0, sx, sy)
        arrive(rnd, FROM_Y, 1, sy)
        push(rnd, DIAGONAL, 1, sy, sx)
        push(rnd, CORE_X, 0, sx, sc)
        push(rnd, CORE_Y, 1, sy, sc)

    def finish_direct(rnd):
        arrive(rnd, FROM_X, 1, sx)
        push(rnd, CORE_X, 1, sx, sc)
        arrive(rnd, FROM_Y, 0, sy)
        push(rnd, CORE_Y, 0, sy, sc)

    def finish_diagonal(rnd):
        for part in range(2):
            arrive(rnd, DIAGONAL, part, sd)
            push(rnd, CORE_DIAGONAL, part, sd, sc)

    def from_core(rnd, kind, shot):
        for part in range(2):
            arrive(rnd, kind, part, shot)

    def twin(shot):
        return shot + 1 - 2 * c

    def drain(rnd):
        from_core(rnd, CORE_OWN, sc)
        from_core(rnd, CORE_X, twin(sx))
        from_core(rnd, CORE_Y, twin(sy))
        from_core(rnd, CORE_DIAGONAL, twin(sd))

    tile = 512

    def chip_product(column, chip, lanes):
        left = [g[part, chip, pl.ds(s * rows, rows), :] for part in range(2)]
        deep = pl.ds(chip * cols, cols)
        right = [g[part, column, deep, lanes] for part in range(2)]
        dot = functools.partial(jnp.dot, preferred_element_type=jnp.float32)
        real = dot(left[0], right[0]) - dot(left[1], right[1])
        imag = dot(left[0], right[1]) + dot(left[1], right[0])
        return real, imag

    def multiply(rnd, chips, first, last):
        column = order[rnd]

        @pl.loop(0, cols // tile)
        def _(t):
            lanes = pl.ds(pl.multiple_of(t * tile, tile), tile)
            wide = pl.ds(pl.multiple_of(column * cols + t * tile, tile), tile)
            real = imag = None
            for chip in chips:
                a, b = chip_product(column, chip, lanes)
                real = a if real is None else real + a
                imag = b if imag is None else imag + b
            if not first:
                real = real + acc[0, :, wide]
                imag = imag + acc[1, :, wide]
            acc[0, :, wide] = real * scale if last else real
            acc[1, :, wide] = imag * scale if last else imag

    def multiply_part(part, chip, last, first=0, deep=cols):
        column = order[-1]

        @pl.loop(0, cols // tile)
        def _(t):
            lanes = pl.ds(pl.multiple_of(t * tile, tile), tile)
            wide = pl.ds(pl.multiple_of(column * cols + t * tile, tile), tile)
            if deep == cols:
                left = [g[p, chip, pl.ds(s * rows, rows), :] for p in range(2)]
            else:
                span = pl.ds(pl.multiple_of(first, rows), rows)
                left = [g[p, chip, pl.ds(s * rows, rows), span] for p in range(2)]
            right = g[part, column, pl.ds(chip * cols + first, deep), lanes]
            dot = functools.partial(jnp.dot, preferred_element_type=jnp.float32)
            a, b = dot(left[part], right), dot(left[1 - part], right)
            real = acc[0, :, wide] + (a if part == 0 else -a)
            imag = acc[1, :, wide] + b
            acc[0, :, wide] = real * scale if last else real
            acc[1, :, wide] = imag * scale if last else imag

    def multiply_shot(part, shot, last):
        multiply_part(part, shot // 2, last, (shot % 2) * rows, rows)

    def deliver(rnd):
        lanes = pl.ds(pl.multiple_of(order[rnd] * cols, cols), cols)
        return pltpu.make_async_copy(acc.at[:, :, lanes], out_ref.at[0, :, :, lanes], out_sem.at[rnd])

    every = range(LINE)

    own = pltpu.make_async_copy(x_ref.at[z], g.at[:, z, pl.ds(s * rows, rows), :], own_sem)

    def toward(peer, begin):
        for part in range(2):
            copy = along_line(peer, part)
            copy.start() if begin else copy.wait_send()

    send_relayed(0)
    toward(others[0], True)
    own.start()
    send_direct(0)

    @pl.when(u == 1)
    def _():
        toward(others[1], True)

    own.wait()
    relay(0)

    @pl.when(u == 1)
    def _():
        toward(others[1], False)
        toward(others[2], True)

    for rnd in range(1, LINE):
        for part in range(2):
            line_arrival(order[rnd], part).wait_recv()
        send_relayed(rnd)
        finish_direct(rnd - 1)
        if rnd == LINE - 1:
            drain(0)
            multiply(0, every, True, True)
            deliver(0).start()
        finish_diagonal(rnd - 1)
        send_direct(rnd)
        if rnd < LINE - 1:

            @pl.when(u == 0)
            def _(peer=others[rnd]):
                toward(peer, True)

        if rnd == LINE - 1:
            drain(1)
            multiply(1, every, True, True)
            deliver(1).start()
        relay(rnd)
    last = LINE - 1
    drain(last - 1)
    multiply(last - 1, every, True, True)
    deliver(last - 1).start()
    from_core(last, CORE_OWN, sc)
    multiply(last, [s // 2], True, False)
    finish_direct(last)
    arrive(last, CORE_X, 0, twin(sx))
    multiply_part(0, sx // 2, False)
    arrive(last, CORE_Y, 1, twin(sy))
    multiply_part(1, sy // 2, False)
    arrive(last, CORE_X, 1, twin(sx))
    multiply_part(1, sx // 2, False)
    arrive(last, CORE_Y, 0, twin(sy))
    multiply_part(0, sy // 2, False)
    finish_diagonal(last)
    for part in range(2):
        multiply_shot(part, sd, False)
    for part in range(2):
        arrive(last, CORE_DIAGONAL, part, twin(sd))
        multiply_shot(part, twin(sd), part == 1)
    deliver(last).start()
    for rnd in range(LINE):
        deliver(rnd).wait()
    for copy in started:
        copy.wait_send()
    toward(others[0], False)
    toward(others[2], False)

    @pl.when(u == 0)
    def _():
        toward(others[1], False)


def in_one_kernel(spectra):
    freqs, parts, rows, cols = spectra.shape
    full = cols * LINE
    return pl.pallas_call(
        functools.partial(kernel, rows, cols, -1.0 / math.sqrt(full)),
        out_shape=jax.ShapeDtypeStruct((1, parts, rows, full), jnp.float32),
        in_specs=[pl.BlockSpec(memory_space=pltpu.HBM)],
        out_specs=pl.BlockSpec(memory_space=pl.ANY),
        scratch_shapes=[
            pltpu.VMEM((parts, LINE, rows * PLANE, cols), jnp.bfloat16),
            pltpu.VMEM((parts, rows, full), jnp.float32),
            pltpu.SemaphoreType.DMA,
            pltpu.SemaphoreType.DMA((LINE,)),
            pltpu.SemaphoreType.DMA((LINE, 2)),
            pltpu.SemaphoreType.DMA((LINE, 2)),
            pltpu.SemaphoreType.DMA((LINE, KINDS)),
            pltpu.SemaphoreType.DMA((LINE, KINDS)),
        ],
        compiler_params=pltpu.CompilerParams(
            collective_id=0, has_side_effects=True, vmem_limit_bytes=28 * 2**20
        ),
    )(pltpu.with_memory_space_constraint(spectra, pltpu.HBM))


def by_collectives(spectra):
    own_rows = lax.all_to_all(spectra, "rcv", split_axis=0, concat_axis=3, tiled=True)
    full = own_rows.shape[3]
    gathered = lax.all_gather(own_rows, "shot", axis=2, tiled=True)
    dot = functools.partial(jnp.einsum, "ang,agv->anv", preferred_element_type=jnp.float32)
    real = dot(own_rows[:, 0], gathered[:, 0]) - dot(own_rows[:, 1], gathered[:, 1])
    imag = dot(own_rows[:, 0], gathered[:, 1]) + dot(own_rows[:, 1], gathered[:, 0])
    return jnp.stack([real, imag], axis=1) * (-1.0 / math.sqrt(full))


def solution(mesh):
    fits = mesh.shape["shot"] == PLANE and mesh.shape["rcv"] == LINE
    return jax.shard_map(
        in_one_kernel if fits else by_collectives,
        mesh=mesh,
        in_specs=(P(None, None, "shot", "rcv"),),
        out_specs=P("rcv", None, "shot", None),
        check_vma=False,
    )
```
